256 devices in a mesh: row: 16 (over z_hi, x), col: 16 (over y, z_lo, core).
Axes of the slice: x: 4, y: 4, z: 8 (z_hi: 4, z_lo: 2; z = z_hi * 2 + z_lo), core: 2. Of those that a mesh axis runs over, the one named last changes fastest.
Arguments:
- coeffs: bfloat16 [16384, 16384], P('row', 'col'), may hold values from -6 to 6
- alpha_blocks: bfloat16 [128, 2, 5, 128, 128], P('row'), may hold values from -0.25 to 0.25
- alpha_cols: int32 [128, 2, 5], P('row'), may hold values from 0 to 7, as said below
- alpha_list: int32 [16], replicated, may hold values from 0 to 15, as said below
- beta_blocks: bfloat16 [128, 2, 5, 128, 128], P('col'), may hold values from -0.25 to 0.25
- beta_cols: int32 [128, 2, 5], P('col'), may hold values from 0 to 7, as said below
- beta_list: int32 [16], replicated, may hold values from 0 to 15, as said below
Outputs:
- sigma: bfloat16 [16384, 16384], P('row', 'col')
The draws below stay inside these ranges and needn't reach their ends.
Inputs may be any that keep to these rules, and one draw needn't show every extreme that they name: `alpha_cols`: within each block row and each of its two tile pairs, the 5 block columns are distinct. `beta_cols`: within each block row and each of its two tile pairs, the 5 block columns are distinct. `alpha_list`: entry i is never i. `beta_list`: entry j is never j.
All inputs are finite; a program needn't handle non-finite values.
Results may differ from the reference program's by a relative error of at most 0.001.
Values may be sent and summed in bfloat16 or wider, within the bound.
No kernel may reach another device: no remote copies, remote signals or barrier semaphores. Data moves between devices by JAX's collectives and lax.ppermute only.
A program may use at most 128 MiB of HBM per device.

```python
import jax
import jax.numpy as jnp
from jax import lax

TILE = 1024
BLK = 128
NBLK = 8
FILL = 5
NA = 16384
NB = 16384


def column_pick(key, rows):
    block_count = TILE // BLK
    filled = 5 * block_count // 8
    column = jnp.arange(block_count, dtype=jnp.int32)
    scores = jax.random.randint(key, (rows, 2, block_count), 0, 1 << 20) * block_count + column
    first_row = jnp.arange(rows, dtype=jnp.int32)[:, None, None] == 0
    first_pair = jnp.arange(2, dtype=jnp.int32)[None, :, None] == 0
    edge = (column == 0) | (column == block_count - 1)
    force = first_row & first_pair & edge[None, None, :]
    scores = jnp.where(force, column - 2 * block_count, scores)
    order = jnp.argsort(scores, axis=-1, stable=True)
    return order[..., :filled].astype(jnp.int32)


def tile_list(key, count):
    position = jnp.arange(count, dtype=jnp.int32)
    shifts = jax.random.randint(jax.random.fold_in(key, 11), (count,), 1, count)
    shifts = jnp.where(position < 2, count - 1, shifts)
    base = (position + shifts) % count
    hottest = jax.random.randint(jax.random.fold_in(key, 12), (), 0, count)
    coin = jax.random.randint(jax.random.fold_in(key, 13), (count,), 0, 2)
    use_hot = (coin == 1) & (position != hottest) & (position >= 2)
    return jnp.where(use_hot, hottest, base).astype(jnp.int32)


def draw_alpha_cols(key, part):
    return column_pick(jax.random.fold_in(key, 1), NA // BLK)


def draw_beta_cols(key, part):
    return column_pick(jax.random.fold_in(key, 2), NB // BLK)


def draw_alpha_list(key, part):
    return tile_list(jax.random.fold_in(key, 3), NA // TILE)


def draw_beta_list(key, part):
    return tile_list(jax.random.fold_in(key, 4), NB // TILE)


def block_scale(key, shape, shards, least, largest):
    gain = 1.0
    for axis_at, parts in shards:
        draws = jax.random.uniform(jax.random.fold_in(jax.random.fold_in(key, 6), axis_at), (parts,), jnp.float32, least / len(shards), largest / len(shards))
        gain = gain * jnp.repeat(jnp.exp(draws), shape[axis_at] // parts).reshape((-1,) + (1,) * (len(shape) - 1 - axis_at))
    return gain


def centred(rng, shape, width, reach, split=(), kind=jnp.bfloat16):
    entries = jax.random.normal(rng, shape, jnp.float32) * width
    if len(split) > 0:
        entries = block_scale(rng, shape, split, -0.22, 0.18) * entries
    return jnp.clip(entries, min=-reach, max=reach).astype(kind)


def setup_inputs(seed: int = 0) -> dict:
    streams_of = jax.random.split(jax.random.key(seed), 8)
    coeffs = centred(streams_of[0], (NA, NB), 1.0, 6.0, ((0, 16), (1, 16)))
    alpha_blocks = centred(streams_of[1], (NA // BLK, 2, FILL, BLK, BLK), (FILL * BLK) ** -0.5, 0.25, ((0, 16),))
    alpha_cols = draw_alpha_cols(jax.random.fold_in(streams_of[7], 71), 0)
    alpha_list = draw_alpha_list(jax.random.fold_in(streams_of[7], 71), 0)
    beta_blocks = centred(streams_of[4], (NB // BLK, 2, FILL, BLK, BLK), (FILL * BLK) ** -0.5, 0.25, ((0, 16),))
    beta_cols = draw_beta_cols(jax.random.fold_in(streams_of[7], 71), 0)
    beta_list = draw_beta_list(jax.random.fold_in(streams_of[7], 71), 0)
    return dict(coeffs=coeffs, alpha_blocks=alpha_blocks, alpha_cols=alpha_cols, alpha_list=alpha_list, beta_blocks=beta_blocks, beta_cols=beta_cols, beta_list=beta_list)


def expand(blocks, cols, strings):
    onehot = (cols[..., None] == jnp.arange(NBLK, dtype=jnp.int32)).astype(jnp.float32)
    dense_rows = jnp.einsum("rskc,rskij->sricj", onehot, blocks.astype(jnp.float32))
    return dense_rows.reshape(2, strings, TILE).astype(jnp.bfloat16)


def reference(coeffs, alpha_blocks, alpha_cols, alpha_list, beta_blocks, beta_cols, beta_list):
    alpha_dense = expand(alpha_blocks, alpha_cols, NA)
    beta_dense = expand(beta_blocks, beta_cols, NB)
    row_count = NA // TILE
    col_count = NB // TILE

    def alpha_tile(tile_index):
        start = (tile_index * TILE).astype(jnp.int32)
        source = (alpha_list[tile_index] * TILE).astype(jnp.int32)
        own_block = lax.dynamic_slice_in_dim(alpha_dense[0], start, TILE, 0)
        listed_block = lax.dynamic_slice_in_dim(alpha_dense[1], start, TILE, 0)
        own_rows = lax.dynamic_slice_in_dim(coeffs, start, TILE, 0)
        listed_rows = lax.dynamic_slice_in_dim(coeffs, source, TILE, 0)
        return (jnp.dot(own_block, own_rows, preferred_element_type=jnp.float32)
                + jnp.dot(listed_block, listed_rows, preferred_element_type=jnp.float32))

    def beta_tile(tile_index):
        start = (tile_index * TILE).astype(jnp.int32)
        source = (beta_list[tile_index] * TILE).astype(jnp.int32)
        own_block = lax.dynamic_slice_in_dim(beta_dense[0], start, TILE, 0)
        listed_block = lax.dynamic_slice_in_dim(beta_dense[1], start, TILE, 0)
        own_cols = lax.dynamic_slice_in_dim(coeffs, start, TILE, 1)
        listed_cols = lax.dynamic_slice_in_dim(coeffs, source, TILE, 1)
        dims = (((1,), (1,)), ((), ()))
        return (lax.dot_general(own_cols, own_block, dims, preferred_element_type=jnp.float32)
                + lax.dot_general(listed_cols, listed_block, dims, preferred_element_type=jnp.float32))

    alpha_term = lax.map(alpha_tile, jnp.arange(row_count, dtype=jnp.int32)).reshape(NA, NB)
    beta_stack = lax.map(beta_tile, jnp.arange(col_count, dtype=jnp.int32))
    beta_term = jnp.transpose(beta_stack, (1, 0, 2)).reshape(NA, NB)
    return (alpha_term + beta_term).astype(jnp.bfloat16)
```

```python
import jax
import jax.numpy as jnp
from jax import lax
from jax.experimental import pallas as pl
from jax.experimental.pallas import tpu as pltpu
from jax.sharding import Mesh
from jax.sharding import PartitionSpec as P


def expand(blocks, cols):
    block_count = blocks.shape[0]
    block_size = blocks.shape[3]
    onehot = (cols[..., None] == jnp.arange(block_count, dtype=jnp.int32)).astype(jnp.bfloat16)
    dense_rows = jnp.einsum("rskc,rskij->sricj", onehot, blocks, preferred_element_type=jnp.float32)
    return dense_rows.reshape(2, block_count * block_size, block_count * block_size).astype(
        jnp.bfloat16
    )


def right_product(left, dense_block):
    return lax.dot_general(
        left, dense_block, (((1,), (1,)), ((), ())), preferred_element_type=jnp.float32
    )


def pick(pools, which, index):
    count = which.shape[0]
    piece = pools[0].shape[1:]

    def kernel(which_ref, index_ref, *refs):
        sources, (out, held, in_sem, out_sem) = refs[: len(pools)], refs[len(pools) :]
        for i in range(count):
            for c, source in enumerate(sources):

                @pl.when(which_ref[i] == c)
                def _():
                    pltpu.make_async_copy(
                        source.at[index_ref[i]], held.at[i], in_sem.at[i]
                    ).start()

        for i in range(count):
            pltpu.make_async_copy(sources[0].at[0], held.at[i], in_sem.at[i]).wait()
            pltpu.make_async_copy(held.at[i], out.at[i], out_sem.at[i]).start()
        for i in range(count):
            pltpu.make_async_copy(held.at[i], out.at[i], out_sem.at[i]).wait()

    return pl.pallas_call(
        kernel,
        out_shape=jax.ShapeDtypeStruct((count,) + piece, pools[0].dtype),
        grid_spec=pltpu.PrefetchScalarGridSpec(
            num_scalar_prefetch=2,
            grid=(1,),
            in_specs=[pl.BlockSpec(memory_space=pl.ANY)] * len(pools),
            out_specs=pl.BlockSpec(memory_space=pl.ANY),
            scratch_shapes=[
                pltpu.VMEM((count,) + piece, pools[0].dtype),
                pltpu.SemaphoreType.DMA((count,)),
                pltpu.SemaphoreType.DMA((count,)),
            ],
        ),
        cost_estimate=pl.CostEstimate(
            flops=0, transcendentals=0, bytes_accessed=4 * count * piece[0] * piece[1]
        ),
    )(which, index, *pools)


def swap(value, axis):
    return lax.ppermute(value, axis, [(0, 1), (1, 0)])


def exchange(value, axis):
    return lax.all_to_all(value, axis, split_axis=0, concat_axis=0, tiled=True)


def shift(value, axis, step):
    count = lax.axis_size(axis)
    return lax.ppermute(value, axis, [(i, (i + step) % count) for i in range(count)])


def shards(coeffs, alpha_blocks, alpha_cols, alpha_list, beta_blocks, beta_cols, beta_list):
    strings = coeffs.shape[0]
    rows = 16
    alpha_pieces = coeffs.reshape(rows, strings // rows, strings)
    beta_pieces = coeffs.reshape(4, strings // 4, strings)
    y = lax.axis_index("y")
    core = lax.axis_index("core")
    z_lo = lax.axis_index("zl")

    near = jnp.stack([beta_pieces[0]] + [shift(beta_pieces[s], "y", s) for s in (1, 2, 3)])
    alpha_held = exchange(alpha_pieces, ("zh", "x"))

    across = swap(near, "zl")
    near_twin = swap(near, "core")
    across_twin = swap(across, "core")

    reach = jnp.arange(4, dtype=jnp.int32)
    column = 2 * z_lo + core
    wanted = jnp.take(beta_list, 4 * ((y + reach) % 4) + column)
    far = ((wanted // 2) % 2 != z_lo).astype(jnp.int32)
    twin = (wanted % 2 != core).astype(jnp.int32)
    beta_out = pick([near, across, near_twin, across_twin], far + 2 * twin, (y - wanted // 4) % 4)
    arrived = [beta_out[:1]] + [shift(beta_out[s : s + 1], "y", s) for s in (1, 2, 3)]
    mine = jnp.take(beta_list, 4 * y + column) // 4
    beta_fetched = pick(arrived, (y - mine - reach) % 4, jnp.zeros_like(reach))
    beta_fetched = beta_fetched.reshape(strings, strings)

    alpha_out = pick([alpha_held], jnp.zeros_like(alpha_list), alpha_list)
    alpha_fetched = exchange(alpha_out, ("zh", "x")).reshape(strings, strings)

    alpha_dense = expand(alpha_blocks, alpha_cols)
    beta_dense = expand(beta_blocks, beta_cols)
    terms = jnp.dot(alpha_dense[0], coeffs, preferred_element_type=jnp.float32)
    terms = terms + right_product(coeffs, beta_dense[0])
    terms = terms + right_product(beta_fetched, beta_dense[1])
    terms = terms + jnp.dot(alpha_dense[1], alpha_fetched, preferred_element_type=jnp.float32)
    return terms.astype(jnp.bfloat16)


def solution(mesh):
    fine = Mesh(mesh.devices.reshape(4, 4, 4, 2, 2), ("zh", "x", "y", "zl", "core"))
    row = ("zh", "x")
    col = ("y", "zl", "core")
    placed = (
        P(row, col),
        P(row, None, None, None, None),
        P(row, None, None),
        P(),
        P(col, None, None, None, None),
        P(col, None, None),
        P(),
    )
    return jax.shard_map(shards, mesh=fine, in_specs=placed, out_specs=P(row, col), check_vma=False)
```

```python
import jax
import jax.numpy as jnp
from jax import lax
from jax.experimental import pallas as pl
from jax.experimental.pallas import tpu as pltpu
from jax.sharding import Mesh
from jax.sharding import PartitionSpec as P


def expand(blocks, cols):
    block_count = blocks.shape[0]
    block_size = blocks.shape[3]
    onehot = (cols[..., None] == jnp.arange(block_count, dtype=jnp.int32)).astype(jnp.bfloat16)
    dense_rows = jnp.einsum("rskc,rskij->sricj", onehot, blocks, preferred_element_type=jnp.float32)
    return dense_rows.reshape(2, block_count * block_size, block_count * block_size).astype(
        jnp.bfloat16
    )


def right_product(left, dense_block):
    return lax.dot_general(
        left, dense_block, (((1,), (1,)), ((), ())), preferred_element_type=jnp.float32
    )


def copy_pieces(pools, table, count, codes):
    piece = pools[0].shape[1:]

    def kernel(table_ref, *refs):
        sources = refs[: len(pools)]
        outs = refs[len(pools) : len(pools) + count]
        held, in_sem, out_sem = refs[len(pools) + count :]
        for i, (pool, index) in enumerate(codes(table_ref)):
            for c, source in enumerate(sources):

                @pl.when(pool == c)
                def _():
                    pltpu.make_async_copy(
                        source.at[jnp.minimum(index, source.shape[0] - 1)], held.at[i], in_sem.at[i]
                    ).start()

        for i in range(count):
            pltpu.make_async_copy(sources[0].at[0], held.at[i], in_sem.at[i]).wait()
            pltpu.make_async_copy(held.at[i], outs[i], out_sem.at[i]).start()
        for i in range(count):
            pltpu.make_async_copy(held.at[i], outs[i], out_sem.at[i]).wait()

    return pl.pallas_call(
        kernel,
        out_shape=[jax.ShapeDtypeStruct(piece, pools[0].dtype)] * count,
        grid_spec=pltpu.PrefetchScalarGridSpec(
            num_scalar_prefetch=1,
            grid=(1,),
            in_specs=[pl.BlockSpec(memory_space=pl.ANY)] * len(pools),
            out_specs=[pl.BlockSpec(memory_space=pl.ANY)] * count,
            scratch_shapes=[
                pltpu.VMEM((count,) + piece, pools[0].dtype),
                pltpu.SemaphoreType.DMA((count,)),
                pltpu.SemaphoreType.DMA((count,)),
            ],
        ),
        cost_estimate=pl.CostEstimate(
            flops=0, transcendentals=0, bytes_accessed=4 * count * piece[0] * piece[1]
        ),
    )(table, *pools)


def gather_pieces(pool, table):
    count = table.shape[0]

    def kernel(table_ref, source, out, held, in_sem, out_sem):
        for i in range(count):
            pltpu.make_async_copy(source.at[table_ref[i]], held.at[i], in_sem.at[i]).start()
        for i in range(count):
            pltpu.make_async_copy(source.at[0], held.at[i], in_sem.at[i]).wait()
            pltpu.make_async_copy(held.at[i], out.at[i], out_sem.at[i]).start()
        for i in range(count):
            pltpu.make_async_copy(held.at[i], out.at[i], out_sem.at[i]).wait()

    return pl.pallas_call(
        kernel,
        out_shape=jax.ShapeDtypeStruct(pool.shape, pool.dtype),
        grid_spec=pltpu.PrefetchScalarGridSpec(
            num_scalar_prefetch=1,
            grid=(1,),
            in_specs=[pl.BlockSpec(memory_space=pl.ANY)],
            out_specs=pl.BlockSpec(memory_space=pl.ANY),
            scratch_shapes=[
                pltpu.VMEM(pool.shape, pool.dtype),
                pltpu.SemaphoreType.DMA((count,)),
                pltpu.SemaphoreType.DMA((count,)),
            ],
        ),
        cost_estimate=pl.CostEstimate(flops=0, transcendentals=0, bytes_accessed=4 * pool.size),
    )(table, pool)


def place():
    return lax.axis_index("y"), lax.axis_index("zl"), lax.axis_index("core")


def crossing(table, source, target):
    present = []
    for k in range(8):
        tile = 4 * (k // 2) + 2 * source + k % 2
        hit = jnp.int32(0)
        for d in range(8):
            hit = hit | (table[4 * (d // 2) + 2 * target + d % 2] == tile).astype(jnp.int32)
        present.append(hit)
    return present


def slot_codes(first):
    def codes(table):
        y, z_lo, core = place()
        found = [(jnp.int32(0), jnp.int32(0))] * 2
        rank = jnp.int32(0)
        for k, hit in enumerate(crossing(table, z_lo, 1 - z_lo)):
            pool, index = (core != k % 2).astype(jnp.int32), (y - k // 2 + 4) % 4
            for j in range(2):
                here = (hit == 1) & (rank == 2 * (first + j) + core)
                found[j] = jnp.where(here, pool, found[j][0]), jnp.where(here, index, found[j][1])
            rank = rank + hit
        return found

    return codes


def send_codes(table):
    y, z_lo, core = place()
    present = crossing(table, 1 - z_lo, z_lo)
    found = []
    for t in range(4):
        wanted = table[4 * ((y + t) % 4) + 2 * z_lo + core]
        tile_y, tile_z, tile_core = wanted // 4, (wanted // 2) % 2, wanted % 2
        rank = jnp.int32(0)
        for k in range(8):
            rank = rank + jnp.where(k < 2 * tile_y + tile_core, present[k], 0)
        slot = rank // 2
        near = tile_z == z_lo
        other = jnp.where(near, tile_core, rank % 2) != core
        pool = jnp.where(near, 0, 2 + 2 * slot) + other.astype(jnp.int32)
        found.append((pool, jnp.where(near, (y - tile_y + 4) % 4, 0)))
    return found


def order_codes(table):
    y, z_lo, core = place()
    mine = table[4 * y + 2 * z_lo + core] // 4
    return [((y - mine - i + 8) % 4, jnp.int32(0)) for i in range(4)]


def swap(value, axis):
    return lax.ppermute(value, axis, [(0, 1), (1, 0)])


def exchange(value, axis):
    return lax.all_to_all(value, axis, split_axis=0, concat_axis=0, tiled=True)


def shift(value, axis, step):
    count = lax.axis_size(axis)
    return lax.ppermute(value, axis, [(i, (i + step) % count) for i in range(count)])


def sigma(coeffs, alpha_blocks, alpha_cols, alpha_list, beta_blocks, beta_cols, beta_list):
    strings = coeffs.shape[0]
    rows = 16
    alpha_pieces = coeffs.reshape(rows, strings // rows, strings)
    beta_pieces = coeffs.reshape(4, strings // 4, strings)

    near = [shift(beta_pieces[s], "y", s) for s in (1, 2, 3)]
    near = jnp.stack([beta_pieces[0]] + near)
    alpha_held = exchange(alpha_pieces, ("zh", "x"))

    near_twin = swap(near, "core")
    slots = copy_pieces([near, near_twin], beta_list, 2, slot_codes(0))
    slots = [swap(slot, "zl")[None] for slot in slots]
    slots = [[slot, swap(slot, "core")] for slot in slots]

    counts = [sum(crossing(beta_list, side, 1 - side)) for side in (0, 1)]

    def carry():
        more = copy_pieces([near, near_twin], beta_list, 2, slot_codes(2))
        more = [swap(slot, "zl")[None] for slot in more]
        return [[slot, swap(slot, "core")] for slot in more]

    def skip():
        return slots

    more = lax.cond(jnp.maximum(counts[0], counts[1]) > 4, carry, skip)
    pools = [near, near_twin] + slots[0] + slots[1] + more[0] + more[1]
    leaving = [piece[None] for piece in copy_pieces(pools, beta_list, 4, send_codes)]
    arrived = leaving[:1] + [shift(leaving[s], "y", s) for s in (1, 2, 3)]
    beta_fetched = copy_pieces(arrived, beta_list, 4, order_codes)

    alpha_out = gather_pieces(alpha_held, alpha_list)
    alpha_fetched = exchange(alpha_out, ("zh", "x")).reshape(strings, strings)

    alpha_dense = expand(alpha_blocks, alpha_cols)
    beta_dense = expand(beta_blocks, beta_cols)
    terms = jnp.dot(alpha_dense[0], coeffs, preferred_element_type=jnp.float32)
    terms = terms + right_product(coeffs, beta_dense[0])
    terms = lax.optimization_barrier(terms)
    terms = terms + right_product(jnp.concatenate(beta_fetched), beta_dense[1])
    terms = lax.optimization_barrier(terms)
    terms = terms + jnp.dot(alpha_dense[1], alpha_fetched, preferred_element_type=jnp.float32)
    return terms.astype(jnp.bfloat16)


def solution(mesh):
    fine = Mesh(mesh.devices.reshape(4, 4, 4, 2, 2), ("zh", "x", "y", "zl", "core"))
    row = ("zh", "x")
    col = ("y", "zl", "core")
    placed = (
        P(row, col),
        P(row, None, None, None, None),
        P(row, None, None),
        P(),
        P(col, None, None, None, None),
        P(col, None, None),
        P(),
    )
    return jax.shard_map(sigma, mesh=fine, in_specs=placed, out_specs=P(row, col), check_vma=False)
```

```python
import jax
import jax.numpy as jnp
from jax import lax
from jax.experimental import pallas as pl
from jax.experimental.pallas import tpu as pltpu
from jax.sharding import Mesh
from jax.sharding import PartitionSpec as P


def fill(dense, blocks, table, pair, transpose):
    dense[...] = jnp.zeros_like(dense)
    size = blocks.shape[-1]
    for row in range(blocks.shape[0]):
        for k in range(blocks.shape[2]):
            column = table[(row * 2 + pair) * blocks.shape[2] + k]
            place = pl.ds(pl.multiple_of(column * size, size), size)
            strip = pl.ds(row * size, size)
            if transpose:
                dense[place, strip] = blocks[row, pair, k].T
            else:
                dense[strip, place] = blocks[row, pair, k]


def own_terms(coeffs, alpha_blocks, alpha_cols, beta_blocks, beta_cols):
    size = coeffs.shape[0]
    step = 256

    def kernel(a_table, b_table, c, a_blocks, b_blocks, terms, a_listed, b_listed, a_own, b_own):
        fill(a_own, a_blocks, a_table, 0, False)
        fill(b_own, b_blocks, b_table, 0, True)
        fill(a_listed, a_blocks, a_table, 1, False)
        fill(b_listed, b_blocks, b_table, 1, True)

        @pl.loop(0, size // step)
        def _(i):
            rows = pl.ds(pl.multiple_of(i * step, step), step)
            terms[rows, :] = jnp.dot(
                a_own[rows, :], c[...], preferred_element_type=jnp.float32
            ) + jnp.dot(c[rows, :], b_own[...], preferred_element_type=jnp.float32)

    square = (size, size)
    whole = pl.BlockSpec(memory_space=pltpu.VMEM)
    return pl.pallas_call(
        kernel,
        out_shape=[
            jax.ShapeDtypeStruct(square, jnp.float32),
            jax.ShapeDtypeStruct(square, jnp.bfloat16),
            jax.ShapeDtypeStruct(square, jnp.bfloat16),
        ],
        in_specs=[pl.BlockSpec(memory_space=pltpu.SMEM)] * 2 + [whole] * 3,
        out_specs=[whole] * 3,
        scratch_shapes=[pltpu.VMEM(square, jnp.bfloat16)] * 2,
        cost_estimate=pl.CostEstimate(
            flops=4 * size**3, transcendentals=0, bytes_accessed=15 * size * size
        ),
    )(alpha_cols.reshape(-1), beta_cols.reshape(-1), coeffs, alpha_blocks, beta_blocks)


def add_beta(table, terms, pieces, dense):
    step, size = pieces[0].shape

    def kernel(table_ref, terms_ref, dense_ref, *refs):
        pieces_ref, out = refs[:-1], refs[-1]
        for i, block in enumerate(order_codes(table_ref)):
            rows = pl.ds(pl.multiple_of(block * step, step), step)
            out[rows, :] = terms_ref[rows, :] + jnp.dot(
                pieces_ref[i][...], dense_ref[...], preferred_element_type=jnp.float32
            )

    whole = pl.BlockSpec(memory_space=pltpu.VMEM)
    return pl.pallas_call(
        kernel,
        out_shape=jax.ShapeDtypeStruct(terms.shape, jnp.float32),
        in_specs=[pl.BlockSpec(memory_space=pltpu.SMEM)] + [whole] * (2 + len(pieces)),
        out_specs=whole,
        input_output_aliases={1: 0},
        cost_estimate=pl.CostEstimate(
            flops=2 * size**3, transcendentals=0, bytes_accessed=12 * size * size
        ),
    )(table, terms, dense, *pieces)


def add_alpha(terms, dense, fetched):
    size = terms.shape[0]
    step = 256

    def kernel(terms_ref, dense_ref, fetched_ref, out):
        product = jnp.dot(dense_ref[...], fetched_ref[...], preferred_element_type=jnp.float32)
        out[...] = (terms_ref[...] + product).astype(out.dtype)

    strip = pl.BlockSpec((size, step), lambda i: (0, i))
    return pl.pallas_call(
        kernel,
        out_shape=jax.ShapeDtypeStruct(terms.shape, fetched.dtype),
        grid=(size // step,),
        in_specs=[strip, pl.BlockSpec((size, size), lambda i: (0, 0)), strip],
        out_specs=strip,
        cost_estimate=pl.CostEstimate(
            flops=2 * size**3, transcendentals=0, bytes_accessed=10 * size * size
        ),
    )(terms, dense, fetched)


def copy_pieces(pools, table, count, codes, tally=False):
    piece = pools[0].shape[1:]

    def kernel(table_ref, *refs):
        sources = refs[: len(pools)]
        outs = refs[len(pools) : len(pools) + count]
        held, in_sem, out_sem = refs[-3:]
        for i, (pool, index) in enumerate(codes(table_ref)):
            for c, source in enumerate(sources):

                @pl.when(pool == c)
                def _():
                    pltpu.make_async_copy(
                        source.at[jnp.minimum(index, source.shape[0] - 1)], held.at[i], in_sem.at[i]
                    ).start()

        if tally:
            sides = [sum(crossing(table_ref, side, 1 - side)) for side in (0, 1)]
            refs[len(pools) + count][0] = jnp.maximum(sides[0], sides[1])
        for i in range(count):
            pltpu.make_async_copy(sources[0].at[0], held.at[i], in_sem.at[i]).wait()
            pltpu.make_async_copy(held.at[i], outs[i], out_sem.at[i]).start()
        for i in range(count):
            pltpu.make_async_copy(held.at[i], outs[i], out_sem.at[i]).wait()

    return pl.pallas_call(
        kernel,
        out_shape=[jax.ShapeDtypeStruct(piece, pools[0].dtype)] * count
        + [jax.ShapeDtypeStruct((1,), jnp.int32)] * tally,
        grid_spec=pltpu.PrefetchScalarGridSpec(
            num_scalar_prefetch=1,
            grid=(1,),
            in_specs=[pl.BlockSpec(memory_space=pl.ANY)] * len(pools),
            out_specs=[pl.BlockSpec(memory_space=pl.ANY)] * count
            + [pl.BlockSpec(memory_space=pltpu.SMEM)] * tally,
            scratch_shapes=[
                pltpu.VMEM((count,) + piece, pools[0].dtype),
                pltpu.SemaphoreType.DMA((count,)),
                pltpu.SemaphoreType.DMA((count,)),
            ],
        ),
        cost_estimate=pl.CostEstimate(
            flops=0, transcendentals=0, bytes_accessed=4 * count * piece[0] * piece[1]
        ),
    )(table, *pools)


def unwritten(count, shape, dtype):
    return pl.pallas_call(
        lambda *refs: None,
        out_shape=[jax.ShapeDtypeStruct(shape, dtype)] * count,
        out_specs=[pl.BlockSpec(memory_space=pl.ANY)] * count,
    )()


def gather_pieces(pool, table):
    count = table.shape[0]

    def kernel(table_ref, source, out, held, in_sem, out_sem):
        for i in range(count):
            pltpu.make_async_copy(source.at[table_ref[i]], held.at[i], in_sem.at[i]).start()
        for i in range(count):
            pltpu.make_async_copy(source.at[0], held.at[i], in_sem.at[i]).wait()
            pltpu.make_async_copy(held.at[i], out.at[i], out_sem.at[i]).start()
        for i in range(count):
            pltpu.make_async_copy(held.at[i], out.at[i], out_sem.at[i]).wait()

    return pl.pallas_call(
        kernel,
        out_shape=jax.ShapeDtypeStruct(pool.shape, pool.dtype),
        grid_spec=pltpu.PrefetchScalarGridSpec(
            num_scalar_prefetch=1,
            grid=(1,),
            in_specs=[pl.BlockSpec(memory_space=pl.ANY)],
            out_specs=pl.BlockSpec(memory_space=pl.ANY),
            scratch_shapes=[
                pltpu.VMEM(pool.shape, pool.dtype),
                pltpu.SemaphoreType.DMA((count,)),
                pltpu.SemaphoreType.DMA((count,)),
            ],
        ),
        cost_estimate=pl.CostEstimate(flops=0, transcendentals=0, bytes_accessed=4 * pool.size),
    )(table, pool)


def place():
    return lax.axis_index("y"), lax.axis_index("zl"), lax.axis_index("core")


def crossing(table, source, target):
    present = []
    for k in range(8):
        tile = 4 * (k // 2) + 2 * source + k % 2
        hit = jnp.int32(0)
        for d in range(8):
            hit = hit | (table[4 * (d // 2) + 2 * target + d % 2] == tile).astype(jnp.int32)
        present.append(hit)
    return present


def slot_codes(first):
    def codes(table):
        y, z_lo, core = place()
        found = [(jnp.int32(0), jnp.int32(0))] * 2
        rank = jnp.int32(0)
        for k, hit in enumerate(crossing(table, z_lo, 1 - z_lo)):
            pool, index = (core != k % 2).astype(jnp.int32), (y - k // 2 + 4) % 4
            for j in range(2):
                here = (hit == 1) & (rank == 2 * (first + j) + core)
                found[j] = jnp.where(here, pool, found[j][0]), jnp.where(here, index, found[j][1])
            rank = rank + hit
        return found

    return codes


def send_codes(table):
    y, z_lo, core = place()
    present = crossing(table, 1 - z_lo, z_lo)
    found = []
    for t in range(4):
        wanted = table[4 * ((y + t) % 4) + 2 * z_lo + core]
        tile_y, tile_z, tile_core = wanted // 4, (wanted // 2) % 2, wanted % 2
        rank = jnp.int32(0)
        for k in range(8):
            rank = rank + jnp.where(k < 2 * tile_y + tile_core, present[k], 0)
        slot = rank // 2
        near = tile_z == z_lo
        other = jnp.where(near, tile_core, rank % 2) != core
        pool = jnp.where(near, 0, 2 + 2 * slot) + other.astype(jnp.int32)
        found.append((pool, jnp.where(near, (y - tile_y + 4) % 4, 0)))
    return found


def order_codes(table):
    y, z_lo, core = place()
    mine = table[4 * y + 2 * z_lo + core] // 4
    return [(y - mine - i + 8) % 4 for i in range(4)]


def swap(value, axis):
    return lax.ppermute(value, axis, [(0, 1), (1, 0)])


def exchange(value, axis):
    return lax.all_to_all(value, axis, split_axis=0, concat_axis=0, tiled=True)


def shift(value, axis, step):
    count = lax.axis_size(axis)
    return lax.ppermute(value, axis, [(i, (i + step) % count) for i in range(count)])


def sigma(coeffs, alpha_blocks, alpha_cols, alpha_list, beta_blocks, beta_cols, beta_list):
    strings = coeffs.shape[0]
    rows = 16
    alpha_pieces = coeffs.reshape(rows, strings // rows, strings)
    beta_pieces = coeffs.reshape(4, strings // 4, strings)

    near = [shift(beta_pieces[s], "y", s) for s in (1, 2, 3)]
    near = jnp.stack([beta_pieces[0]] + near)
    alpha_held = exchange(alpha_pieces, ("zh", "x"))

    near_twin = swap(near, "core")
    *slots, most = copy_pieces([near, near_twin], beta_list, 2, slot_codes(0), tally=True)
    slots = [swap(slot, "zl")[None] for slot in slots]

    def carry():
        more = copy_pieces([near, near_twin], beta_list, 2, slot_codes(2))
        more = [swap(slot, "zl") for slot in more]
        return tuple(more + [swap(slot, "core") for slot in more])

    def skip():
        return tuple(unwritten(4, near.shape[1:], near.dtype))

    more = lax.cond(most[0] > 4, carry, skip)
    pools = [near, near_twin]
    for slot in slots:
        pools += [slot, swap(slot, "core")]
    for own, twin in zip(more[:2], more[2:]):
        pools += [own[None], twin[None]]
    leaving = copy_pieces(pools, beta_list, 4, send_codes)
    arrived = [leaving[0]] + [shift(leaving[s], "y", s) for s in (1, 2, 3)]

    alpha_out = gather_pieces(alpha_held, alpha_list)
    alpha_fetched = exchange(alpha_out, ("zh", "x")).reshape(strings, strings)

    terms, alpha_dense, beta_dense = own_terms(
        coeffs, alpha_blocks, alpha_cols, beta_blocks, beta_cols
    )
    terms = add_beta(beta_list, terms, arrived, beta_dense)
    return add_alpha(terms, alpha_dense, alpha_fetched)


def solution(mesh):
    fine = Mesh(mesh.devices.reshape(4, 4, 4, 2, 2), ("zh", "x", "y", "zl", "core"))
    row = ("zh", "x")
    col = ("y", "zl", "core")
    placed = (
        P(row, col),
        P(row, None, None, None, None),
        P(row, None, None),
        P(),
        P(col, None, None, None, None),
        P(col, None, None),
        P(),
    )
    return jax.shard_map(sigma, mesh=fine, in_specs=placed, out_specs=P(row, col), check_vma=False)
```

```python
import jax
import jax.numpy as jnp
from jax import lax
from jax.experimental import pallas as pl
from jax.experimental.pallas import tpu as pltpu
from jax.sharding import Mesh
from jax.sharding import PartitionSpec as P


def fill(dense, blocks, table, pair, transpose):
    dense[...] = jnp.zeros_like(dense)
    size = blocks.shape[-1]
    for row in range(blocks.shape[0]):
        for k in range(blocks.shape[2]):
            column = table[(row * 2 + pair) * blocks.shape[2] + k]
            place = pl.ds(pl.multiple_of(column * size, size), size)
            strip = pl.ds(row * size, size)
            if transpose:
                dense[place, strip] = blocks[row, pair, k].T
            else:
                dense[strip, place] = blocks[row, pair, k]


def own_terms(coeffs, alpha_blocks, alpha_cols, beta_blocks, beta_cols):
    size = coeffs.shape[0]
    step = 256

    def kernel(a_table, b_table, c, a_blocks, b_blocks, terms, a_listed, b_listed, a_own, b_own):
        fill(a_own, a_blocks, a_table, 0, False)
        fill(b_own, b_blocks, b_table, 0, True)
        fill(a_listed, a_blocks, a_table, 1, False)
        fill(b_listed, b_blocks, b_table, 1, True)

        @pl.loop(0, size // step)
        def _(i):
            rows = pl.ds(pl.multiple_of(i * step, step), step)
            terms[rows, :] = jnp.dot(
                a_own[rows, :], c[...], preferred_element_type=jnp.float32
            ) + jnp.dot(c[rows, :], b_own[...], preferred_element_type=jnp.float32)

    square = (size, size)
    whole = pl.BlockSpec(memory_space=pltpu.VMEM)
    return pl.pallas_call(
        kernel,
        out_shape=[
            jax.ShapeDtypeStruct(square, jnp.float32),
            jax.ShapeDtypeStruct(square, jnp.bfloat16),
            jax.ShapeDtypeStruct(square, jnp.bfloat16),
        ],
        in_specs=[pl.BlockSpec(memory_space=pltpu.SMEM)] * 2 + [whole] * 3,
        out_specs=[whole] * 3,
        scratch_shapes=[pltpu.VMEM(square, jnp.bfloat16)] * 2,
        cost_estimate=pl.CostEstimate(
            flops=4 * size**3, transcendentals=0, bytes_accessed=15 * size * size
        ),
    )(alpha_cols.reshape(-1), beta_cols.reshape(-1), coeffs, alpha_blocks, beta_blocks)


def add_beta(facts, terms, pieces, dense):
    step, size = pieces[0].shape

    def kernel(facts_ref, terms_ref, dense_ref, *refs):
        out = refs[-1]
        for i, piece in enumerate(refs[:-1]):

            @pl.when(pl.program_id(0) == i)
            def _():
                out[...] = terms_ref[...] + jnp.dot(
                    piece[...], dense_ref[...], preferred_element_type=jnp.float32
                )

    rows = pl.BlockSpec((step, size), lambda i, facts: (facts[1 + i], 0))
    piece = pl.BlockSpec((step, size), lambda i, facts: (0, 0))
    return pl.pallas_call(
        kernel,
        out_shape=jax.ShapeDtypeStruct(terms.shape, jnp.float32),
        grid_spec=pltpu.PrefetchScalarGridSpec(
            num_scalar_prefetch=1,
            grid=(len(pieces),),
            in_specs=[rows, pl.BlockSpec((size, size), lambda i, facts: (0, 0))]
            + [piece] * len(pieces),
            out_specs=rows,
        ),
        input_output_aliases={1: 0},
        cost_estimate=pl.CostEstimate(
            flops=2 * size**3, transcendentals=0, bytes_accessed=12 * size * size
        ),
    )(facts, terms, dense, *pieces)


def add_alpha(terms, dense, fetched):
    size = terms.shape[0]
    step = size // 2

    def kernel(terms_ref, dense_ref, fetched_ref, out):
        product = jnp.dot(dense_ref[...], fetched_ref[...], preferred_element_type=jnp.float32)
        out[...] = (terms_ref[...] + product).astype(out.dtype)

    rows = pl.BlockSpec((step, size), lambda i: (i, 0))
    return pl.pallas_call(
        kernel,
        out_shape=jax.ShapeDtypeStruct(terms.shape, fetched.dtype),
        grid=(size // step,),
        in_specs=[rows, rows, pl.BlockSpec((size, size), lambda i: (0, 0))],
        out_specs=rows,
        cost_estimate=pl.CostEstimate(
            flops=2 * size**3, transcendentals=0, bytes_accessed=10 * size * size
        ),
    )(terms, dense, fetched)


def copy_pieces(parts, table, count, codes, tally=False):
    rows, width = parts[0][0].shape
    kind = parts[0][0].dtype
    piece = (len(parts) * rows, width)
    flat = sum((list(part) for part in parts), [])

    def kernel(table_ref, *refs):
        outs = refs[len(flat) : len(flat) + count]
        held, in_sem, out_sem = refs[-3:]
        for i, pool in enumerate(codes(table_ref)):
            for c in range(len(parts[0])):

                @pl.when(pool == c)
                def _():
                    for h in range(len(parts)):
                        pltpu.make_async_copy(
                            refs[h * len(parts[0]) + c],
                            held.at[i, pl.ds(h * rows, rows)],
                            in_sem.at[i, h],
                        ).start()

        if tally:
            facts = refs[len(flat) + count]
            sides = [sum(crossing(table_ref, side, 1 - side)) for side in (0, 1)]
            facts[0] = jnp.maximum(sides[0], sides[1])
            for i, block in enumerate(order_codes(table_ref)):
                facts[1 + i] = block
        for i in range(count):
            for h in range(len(parts)):
                pltpu.make_async_copy(
                    refs[0], held.at[i, pl.ds(h * rows, rows)], in_sem.at[i, h]
                ).wait()
            pltpu.make_async_copy(held.at[i], outs[i], out_sem.at[i]).start()
        for i in range(count):
            pltpu.make_async_copy(held.at[i], outs[i], out_sem.at[i]).wait()

    return pl.pallas_call(
        kernel,
        out_shape=[jax.ShapeDtypeStruct(piece, kind)] * count
        + [jax.ShapeDtypeStruct((5,), jnp.int32)] * tally,
        in_specs=[pl.BlockSpec(memory_space=pltpu.SMEM)]
        + [pl.BlockSpec(memory_space=pl.ANY)] * len(flat),
        out_specs=[pl.BlockSpec(memory_space=pl.ANY)] * count
        + [pl.BlockSpec(memory_space=pltpu.SMEM)] * tally,
        scratch_shapes=[
            pltpu.VMEM((count,) + piece, kind),
            pltpu.SemaphoreType.DMA((count, len(parts))),
            pltpu.SemaphoreType.DMA((count,)),
        ],
        cost_estimate=pl.CostEstimate(
            flops=0, transcendentals=0, bytes_accessed=4 * count * piece[0] * piece[1]
        ),
    )(table, *flat)


def unwritten(count, shape, dtype):
    return pl.pallas_call(
        lambda *refs: None,
        out_shape=[jax.ShapeDtypeStruct(shape, dtype)] * count,
        out_specs=[pl.BlockSpec(memory_space=pl.ANY)] * count,
    )()


def gather_pieces(pool, table):
    count = table.shape[0]

    def kernel(table_ref, source, out, held, in_sem, out_sem):
        for i in range(count):
            pltpu.make_async_copy(source.at[table_ref[i]], held.at[i], in_sem.at[i]).start()
        for i in range(count):
            pltpu.make_async_copy(source.at[0], held.at[i], in_sem.at[i]).wait()
            pltpu.make_async_copy(held.at[i], out.at[i], out_sem.at[i]).start()
        for i in range(count):
            pltpu.make_async_copy(held.at[i], out.at[i], out_sem.at[i]).wait()

    return pl.pallas_call(
        kernel,
        out_shape=jax.ShapeDtypeStruct(pool.shape, pool.dtype),
        grid_spec=pltpu.PrefetchScalarGridSpec(
            num_scalar_prefetch=1,
            grid=(1,),
            in_specs=[pl.BlockSpec(memory_space=pl.ANY)],
            out_specs=pl.BlockSpec(memory_space=pl.ANY),
            scratch_shapes=[
                pltpu.VMEM(pool.shape, pool.dtype),
                pltpu.SemaphoreType.DMA((count,)),
                pltpu.SemaphoreType.DMA((count,)),
            ],
        ),
        cost_estimate=pl.CostEstimate(flops=0, transcendentals=0, bytes_accessed=4 * pool.size),
    )(table, pool)


def place():
    return lax.axis_index("y"), lax.axis_index("zl"), lax.axis_index("core")


def crossing(table, source, target):
    present = []
    for k in range(8):
        tile = 4 * (k // 2) + 2 * source + k % 2
        hit = jnp.int32(0)
        for d in range(8):
            hit = hit | (table[4 * (d // 2) + 2 * target + d % 2] == tile).astype(jnp.int32)
        present.append(hit)
    return present


def slot_codes(first):
    def codes(table):
        y, z_lo, core = place()
        found = [jnp.int32(0)] * 2
        rank = jnp.int32(0)
        for k, hit in enumerate(crossing(table, z_lo, 1 - z_lo)):
            pool = 4 * (core != k % 2).astype(jnp.int32) + (y - k // 2 + 4) % 4
            for j in range(2):
                here = (hit == 1) & (rank == 2 * (first + j) + core)
                found[j] = jnp.where(here, pool, found[j])
            rank = rank + hit
        return found

    return codes


def send_codes(table):
    y, z_lo, core = place()
    present = crossing(table, 1 - z_lo, z_lo)
    found = []
    for t in range(4):
        wanted = table[4 * ((y + t) % 4) + 2 * z_lo + core]
        tile_y, tile_z, tile_core = wanted // 4, (wanted // 2) % 2, wanted % 2
        rank = jnp.int32(0)
        for k in range(8):
            rank = rank + jnp.where(k < 2 * tile_y + tile_core, present[k], 0)
        near = 4 * (tile_core != core).astype(jnp.int32) + (y - tile_y + 4) % 4
        far = 8 + 2 * (rank // 2) + (rank % 2 != core).astype(jnp.int32)
        found.append(jnp.where(tile_z == z_lo, near, far))
    return found


def order_codes(table):
    y, z_lo, core = place()
    mine = table[4 * y + 2 * z_lo + core] // 4
    return [(y - mine - i + 8) % 4 for i in range(4)]


def swap(value, axis):
    return lax.ppermute(value, axis, [(0, 1), (1, 0)])


def exchange(value, axis):
    return lax.all_to_all(value, axis, split_axis=0, concat_axis=0, tiled=True)


def shift(value, axis, step):
    count = lax.axis_size(axis)
    return lax.ppermute(value, axis, [(i, (i + step) % count) for i in range(count)])


def sigma(coeffs, alpha_blocks, alpha_cols, alpha_list, beta_blocks, beta_cols, beta_list):
    strings = coeffs.shape[0]
    rows = 16
    alpha_pieces = coeffs.reshape(rows, strings // rows, strings)
    beta_pieces = coeffs.reshape(4, 2, strings // 8, strings)

    near = []
    for h in range(2):
        near.append([shift(beta_pieces[s, h], "y", s) for s in (1, 2, 3)])
    alpha_held = exchange(alpha_pieces, ("zh", "x"))

    slots = []
    for h in range(2):
        near[h] = [beta_pieces[0, h]] + near[h]
        near[h] = near[h] + [swap(piece, "core") for piece in near[h]]
        *sent, facts = copy_pieces([near[h]], beta_list, 2, slot_codes(0), tally=True)
        slots.append([swap(slot, "zl") for slot in sent])

    def carry():
        more = []
        for h in range(2):
            sent = copy_pieces([near[h]], beta_list, 2, slot_codes(2))
            sent = [swap(slot, "zl") for slot in sent]
            more += sent + [swap(slot, "core") for slot in sent]
        return tuple(more)

    def skip():
        return tuple(unwritten(8, near[0][0].shape, near[0][0].dtype))

    more = lax.cond(facts[0] > 4, carry, skip)
    parts = []
    for h in range(2):
        pools = list(near[h])
        for slot in slots[h]:
            pools += [slot, swap(slot, "core")]
        for j in range(2):
            pools += [more[4 * h + j], more[4 * h + 2 + j]]
        parts.append(pools)
    leaving = copy_pieces(parts, beta_list, 4, send_codes)
    arrived = [leaving[0]] + [shift(leaving[s], "y", s) for s in (1, 2, 3)]

    alpha_out = gather_pieces(alpha_held, alpha_list)
    alpha_fetched = exchange(alpha_out, ("zh", "x")).reshape(strings, strings)

    terms, alpha_dense, beta_dense = own_terms(
        coeffs, alpha_blocks, alpha_cols, beta_blocks, beta_cols
    )
    terms = add_beta(facts, terms, arrived, beta_dense)
    return add_alpha(terms, alpha_dense, alpha_fetched)


def solution(mesh):
    fine = Mesh(mesh.devices.reshape(4, 4, 4, 2, 2), ("zh", "x", "y", "zl", "core"))
    row = ("zh", "x")
    col = ("y", "zl", "core")
    placed = (
        P(row, col),
        P(row, None, None, None, None),
        P(row, None, None),
        P(),
        P(col, None, None, None, None),
        P(col, None, None),
        P(),
    )
    return jax.shard_map(sigma, mesh=fine, in_specs=placed, out_specs=P(row, col), check_vma=False)
```

```python
import jax
import jax.numpy as jnp
from jax import lax
from jax.experimental import pallas as pl
from jax.experimental.pallas import tpu as pltpu
from jax.sharding import Mesh
from jax.sharding import PartitionSpec as P


def fill(dense, blocks, table, pair, transpose):
    dense[...] = jnp.zeros_like(dense)
    size = blocks.shape[-1]
    for row in range(blocks.shape[0]):
        for k in range(blocks.shape[2]):
            column = table[(row * 2 + pair) * blocks.shape[2] + k]
            place = pl.ds(pl.multiple_of(column * size, size), size)
            strip = pl.ds(row * size, size)
            if transpose:
                dense[place, strip] = blocks[row, pair, k].T
            else:
                dense[strip, place] = blocks[row, pair, k]


def own_terms(coeffs, alpha_blocks, alpha_cols, beta_blocks, beta_cols):
    size = coeffs.shape[0]
    step = 256

    def kernel(a_table, b_table, c, a_blocks, b_blocks, terms, a_listed, b_listed, a_own, b_own):
        fill(a_own, a_blocks, a_table, 0, False)
        fill(b_own, b_blocks, b_table, 0, True)
        fill(a_listed, a_blocks, a_table, 1, False)
        fill(b_listed, b_blocks, b_table, 1, True)

        @pl.loop(0, size // step)
        def _(i):
            rows = pl.ds(pl.multiple_of(i * step, step), step)
            terms[rows, :] = jnp.dot(
                a_own[rows, :], c[...], preferred_element_type=jnp.float32
            ) + jnp.dot(c[rows, :], b_own[...], preferred_element_type=jnp.float32)

    square = (size, size)
    whole = pl.BlockSpec(memory_space=pltpu.VMEM)
    return pl.pallas_call(
        kernel,
        out_shape=[
            jax.ShapeDtypeStruct(square, jnp.float32),
            jax.ShapeDtypeStruct(square, jnp.bfloat16),
            jax.ShapeDtypeStruct(square, jnp.bfloat16),
        ],
        in_specs=[pl.BlockSpec(memory_space=pltpu.SMEM)] * 2 + [whole] * 3,
        out_specs=[whole] * 3,
        scratch_shapes=[pltpu.VMEM(square, jnp.bfloat16)] * 2,
        cost_estimate=pl.CostEstimate(
            flops=4 * size**3, transcendentals=0, bytes_accessed=15 * size * size
        ),
    )(alpha_cols.reshape(-1), beta_cols.reshape(-1), coeffs, alpha_blocks, beta_blocks)


def add_beta(facts, terms, pieces, dense, first):
    step, size = pieces[0].shape

    def kernel(facts_ref, terms_ref, dense_ref, *refs):
        out = refs[-1]
        for i, piece in enumerate(refs[:-1]):

            @pl.when(pl.program_id(0) == i)
            def _():
                out[...] = terms_ref[...] + jnp.dot(
                    piece[...], dense_ref[...], preferred_element_type=jnp.float32
                )

    rows = pl.BlockSpec((step, size), lambda i, facts: (facts[1 + first + i], 0))
    piece = pl.BlockSpec((step, size), lambda i, facts: (0, 0))
    return pl.pallas_call(
        kernel,
        out_shape=jax.ShapeDtypeStruct(terms.shape, jnp.float32),
        grid_spec=pltpu.PrefetchScalarGridSpec(
            num_scalar_prefetch=1,
            grid=(len(pieces),),
            in_specs=[rows, pl.BlockSpec((size, size), lambda i, facts: (0, 0))]
            + [piece] * len(pieces),
            out_specs=rows,
        ),
        input_output_aliases={1: 0},
        cost_estimate=pl.CostEstimate(
            flops=2 * len(pieces) * step * size * size,
            transcendentals=0,
            bytes_accessed=12 * len(pieces) * step * size,
        ),
    )(facts, terms, dense, *pieces)


def add_alpha(terms, dense, fetched):
    size = terms.shape[0]
    step = size // 2

    def kernel(terms_ref, dense_ref, fetched_ref, out):
        product = jnp.dot(dense_ref[...], fetched_ref[...], preferred_element_type=jnp.float32)
        out[...] = (terms_ref[...] + product).astype(out.dtype)

    rows = pl.BlockSpec((step, size), lambda i: (i, 0))
    return pl.pallas_call(
        kernel,
        out_shape=jax.ShapeDtypeStruct(terms.shape, fetched.dtype),
        grid=(size // step,),
        in_specs=[rows, rows, pl.BlockSpec((size, size), lambda i: (0, 0))],
        out_specs=rows,
        cost_estimate=pl.CostEstimate(
            flops=2 * size**3, transcendentals=0, bytes_accessed=10 * size * size
        ),
    )(terms, dense, fetched)


def copy_pieces(parts, table, count, codes, tally=False):
    rows, width = parts[0][0].shape
    kind = parts[0][0].dtype
    piece = (len(parts) * rows, width)
    flat = sum((list(part) for part in parts), [])

    def kernel(table_ref, *refs):
        outs = refs[len(flat) : len(flat) + count]
        held, in_sem, out_sem = refs[-3:]
        for i, pool in enumerate(codes(table_ref)):
            for c in range(len(parts[0])):

                @pl.when(pool == c)
                def _():
                    for h in range(len(parts)):
                        pltpu.make_async_copy(
                            refs[h * len(parts[0]) + c],
                            held.at[i, pl.ds(h * rows, rows)],
                            in_sem.at[i, h],
                        ).start()

        if tally:
            facts = refs[len(flat) + count]
            sides = [sum(crossing(table_ref, side, 1 - side)) for side in (0, 1)]
            facts[0] = jnp.maximum(sides[0], sides[1])
            for i, block in enumerate(order_codes(table_ref)):
                facts[1 + i] = block
        for i in range(count):
            for h in range(len(parts)):
                pltpu.make_async_copy(
                    refs[0], held.at[i, pl.ds(h * rows, rows)], in_sem.at[i, h]
                ).wait()
            pltpu.make_async_copy(held.at[i], outs[i], out_sem.at[i]).start()
        for i in range(count):
            pltpu.make_async_copy(held.at[i], outs[i], out_sem.at[i]).wait()

    return pl.pallas_call(
        kernel,
        out_shape=[jax.ShapeDtypeStruct(piece, kind)] * count
        + [jax.ShapeDtypeStruct((5,), jnp.int32)] * tally,
        in_specs=[pl.BlockSpec(memory_space=pltpu.SMEM)]
        + [pl.BlockSpec(memory_space=pl.ANY)] * len(flat),
        out_specs=[pl.BlockSpec(memory_space=pl.ANY)] * count
        + [pl.BlockSpec(memory_space=pltpu.SMEM)] * tally,
        scratch_shapes=[
            pltpu.VMEM((count,) + piece, kind),
            pltpu.SemaphoreType.DMA((count, len(parts))),
            pltpu.SemaphoreType.DMA((count,)),
        ],
        cost_estimate=pl.CostEstimate(
            flops=0, transcendentals=0, bytes_accessed=4 * count * piece[0] * piece[1]
        ),
    )(table, *flat)


def unwritten(count, shape, dtype):
    return pl.pallas_call(
        lambda *refs: None,
        out_shape=[jax.ShapeDtypeStruct(shape, dtype)] * count,
        out_specs=[pl.BlockSpec(memory_space=pl.ANY)] * count,
    )()


def gather_pieces(pool, table):
    count = table.shape[0]

    def kernel(table_ref, source, out, held, in_sem, out_sem):
        for i in range(count):
            pltpu.make_async_copy(source.at[table_ref[i]], held.at[i], in_sem.at[i]).start()
        for i in range(count):
            pltpu.make_async_copy(source.at[0], held.at[i], in_sem.at[i]).wait()
            pltpu.make_async_copy(held.at[i], out.at[i], out_sem.at[i]).start()
        for i in range(count):
            pltpu.make_async_copy(held.at[i], out.at[i], out_sem.at[i]).wait()

    return pl.pallas_call(
        kernel,
        out_shape=jax.ShapeDtypeStruct(pool.shape, pool.dtype),
        grid_spec=pltpu.PrefetchScalarGridSpec(
            num_scalar_prefetch=1,
            grid=(1,),
            in_specs=[pl.BlockSpec(memory_space=pl.ANY)],
            out_specs=pl.BlockSpec(memory_space=pl.ANY),
            scratch_shapes=[
                pltpu.VMEM(pool.shape, pool.dtype),
                pltpu.SemaphoreType.DMA((count,)),
                pltpu.SemaphoreType.DMA((count,)),
            ],
        ),
        cost_estimate=pl.CostEstimate(flops=0, transcendentals=0, bytes_accessed=4 * pool.size),
    )(table, pool)


def place():
    return lax.axis_index("y"), lax.axis_index("zl"), lax.axis_index("core")


def crossing(table, source, target):
    present = []
    for k in range(8):
        tile = 4 * (k // 2) + 2 * source + k % 2
        hit = jnp.int32(0)
        for d in range(8):
            hit = hit | (table[4 * (d // 2) + 2 * target + d % 2] == tile).astype(jnp.int32)
        present.append(hit)
    return present


def slot_codes(first):
    def codes(table):
        y, z_lo, core = place()
        found = [jnp.int32(0)] * 2
        rank = jnp.int32(0)
        for k, hit in enumerate(crossing(table, z_lo, 1 - z_lo)):
            pool = 4 * (core != k % 2).astype(jnp.int32) + (y - k // 2 + 4) % 4
            for j in range(2):
                here = (hit == 1) & (rank == 2 * (first + j) + core)
                found[j] = jnp.where(here, pool, found[j])
            rank = rank + hit
        return found

    return codes


def send_codes(table):
    y, z_lo, core = place()
    present = crossing(table, 1 - z_lo, z_lo)
    found = []
    for t in range(4):
        wanted = table[4 * ((y + t) % 4) + 2 * z_lo + core]
        tile_y, tile_z, tile_core = wanted // 4, (wanted // 2) % 2, wanted % 2
        rank = jnp.int32(0)
        for k in range(8):
            rank = rank + jnp.where(k < 2 * tile_y + tile_core, present[k], 0)
        near = 4 * (tile_core != core).astype(jnp.int32) + (y - tile_y + 4) % 4
        far = 8 + 2 * (rank // 2) + (rank % 2 != core).astype(jnp.int32)
        found.append(jnp.where(tile_z == z_lo, near, far))
    return found


def order_codes(table):
    y, z_lo, core = place()
    mine = table[4 * y + 2 * z_lo + core] // 4
    return [(y - mine - i + 8) % 4 for i in range(4)]


def swap(value, axis):
    return lax.ppermute(value, axis, [(0, 1), (1, 0)])


def exchange(value, axis):
    return lax.all_to_all(value, axis, split_axis=0, concat_axis=0, tiled=True)


def shift(value, axis, step):
    count = lax.axis_size(axis)
    return lax.ppermute(value, axis, [(i, (i + step) % count) for i in range(count)])


def sigma(coeffs, alpha_blocks, alpha_cols, alpha_list, beta_blocks, beta_cols, beta_list):
    strings = coeffs.shape[0]
    rows = 16
    alpha_pieces = coeffs.reshape(rows, strings // rows, strings)
    beta_pieces = coeffs.reshape(4, 2, strings // 8, strings)

    near = []
    for h in range(2):
        near.append([shift(beta_pieces[s, h], "y", s) for s in (1, 2, 3)])
    alpha_held = exchange(alpha_pieces, ("zh", "x"))

    slots = []
    for h in range(2):
        near[h] = [beta_pieces[0, h]] + near[h]
        near[h] = near[h] + [swap(piece, "core") for piece in near[h]]
        *sent, facts = copy_pieces([near[h]], beta_list, 2, slot_codes(0), tally=True)
        slots.append([swap(slot, "zl") for slot in sent])

    def carry():
        more = []
        for h in range(2):
            sent = copy_pieces([near[h]], beta_list, 2, slot_codes(2))
            sent = [swap(slot, "zl") for slot in sent]
            more += sent + [swap(slot, "core") for slot in sent]
        return tuple(more)

    def skip():
        return tuple(unwritten(8, near[0][0].shape, near[0][0].dtype))

    more = lax.cond(facts[0] > 4, carry, skip)
    parts = []
    for h in range(2):
        pools = list(near[h])
        for slot in slots[h]:
            pools += [slot, swap(slot, "core")]
        for j in range(2):
            pools += [more[4 * h + j], more[4 * h + 2 + j]]
        parts.append(pools)
    leaving = copy_pieces(parts, beta_list, 4, send_codes)
    beside = shift(leaving[1], "y", 1)
    late = [shift(leaving[2], "y", 2)]
    late.append(shift(leaving[3], "y", 3))

    alpha_out = gather_pieces(alpha_held, alpha_list)
    alpha_fetched = exchange(alpha_out, ("zh", "x")).reshape(strings, strings)

    terms, alpha_dense, beta_dense = own_terms(
        coeffs, alpha_blocks, alpha_cols, beta_blocks, beta_cols
    )
    terms = add_beta(facts, terms, [leaving[0], beside], beta_dense, 0)
    terms = add_beta(facts, terms, late, beta_dense, 2)
    return add_alpha(terms, alpha_dense, alpha_fetched)


def solution(mesh):
    fine = Mesh(mesh.devices.reshape(4, 4, 4, 2, 2), ("zh", "x", "y", "zl", "core"))
    row = ("zh", "x")
    col = ("y", "zl", "core")
    placed = (
        P(row, col),
        P(row, None, None, None, None),
        P(row, None, None),
        P(),
        P(col, None, None, None, None),
        P(col, None, None),
        P(),
    )
    return jax.shard_map(sigma, mesh=fine, in_specs=placed, out_specs=P(row, col), check_vma=False)
```
